32 devices in a mesh: prow: 4 (over y, x), pcol: 8 (over z, core).
Axes of the slice: x: 2, y: 2, z: 4, core: 2. Of those that a mesh axis runs over, the one named last changes fastest.
Arguments:
- matrix: float32 [12288, 12288], P('prow', 'pcol'), may hold values from -6 to 6, as said below
- reflectors: float32 [12288, 512], P('prow'), may hold values from -0.0546875 to 0.0546875
- factors: float32 [2, 256, 256], replicated, may hold values from -0.25 to 2, as said below
Outputs:
- updated: float32 [12288, 12288], P('prow', 'pcol')
The draws below stay inside these ranges and needn't reach their ends.
Inputs may be any that keep to these rules, and one draw needn't show every extreme that they name: `matrix`: symmetric: entry (i, j) equals entry (j, i). `factors`: each of the 2 blocks is upper triangular with diagonal entries between 1 and 2.
All inputs are finite; a program needn't handle non-finite values.
Results may differ from the reference program's by a relative error of at most 0.0001.
Values sent between devices are 32-bit elements; how exact they have to be, the bound alone decides.
No kernel may reach another device: no remote copies, remote signals or barrier semaphores. Data moves between devices by JAX's collectives and lax.ppermute only.
A program may use at most 128 MiB of HBM per device.

```python
import jax
import jax.numpy as jnp
from jax import lax

N = 12288
NB = 256
PANELS = 2


def draw_matrix(key, part):
    value_key = jax.random.fold_in(key, 11)
    values = jnp.clip(jax.random.normal(value_key, (N, N), jnp.float32), -4.0, 4.0)
    return (values + values.T) * 0.7071


def draw_factors(key, part):
    diag_key = jax.random.fold_in(key, 21)
    upper_key = jax.random.fold_in(key, 22)
    upper = jnp.clip(0.05 * jax.random.normal(upper_key, (PANELS, NB, NB), jnp.float32), -0.25, 0.25)
    diagonal = jax.random.uniform(diag_key, (PANELS, NB), jnp.float32, 1.0, 2.0)
    row_ids = lax_iota_rows()
    above = (row_ids[1][None, :, :] > row_ids[0][None, :, :]).astype(jnp.float32)
    same = (row_ids[1][None, :, :] == row_ids[0][None, :, :]).astype(jnp.float32)
    return upper * above + same * diagonal[:, :, None]


def lax_iota_rows():
    rows_ids = jnp.arange(NB)[:, None] * jnp.ones((1, NB), jnp.int32)
    cols_ids = jnp.arange(NB)[None, :] * jnp.ones((NB, 1), jnp.int32)
    return (rows_ids, cols_ids)


def levels(stream_key, shape, shards, least, largest):
    level = 1.0
    for position, shards_of in shards:
        steps = jax.random.uniform(jax.random.fold_in(jax.random.fold_in(stream_key, 6), position), (shards_of,), jnp.float32, least / len(shards), largest / len(shards))
        level = level * jnp.repeat(jnp.exp(steps), shape[position] // shards_of).reshape((-1,) + (1,) * (len(shape) - 1 - position))
    return level


def gaussian(rng, extent, deviation, limit, split=(), kind=jnp.bfloat16):
    factor_of = levels(rng, extent, split, -0.22, 0.18) if split else 1.0
    drawn = jax.random.normal(rng, extent, jnp.float32) * deviation * factor_of
    return jnp.minimum(jnp.maximum(drawn, -limit), limit).astype(kind)


def setup_inputs(seed: int = 0) -> dict:
    splits = jax.random.split(jax.random.key(seed), 4)
    return {
        "matrix": draw_matrix(jax.random.fold_in(splits[3], 71), 0),
        "reflectors": gaussian(splits[1], (N, PANELS * NB), N ** -0.5, 0.0546875, ((0, 4),), jnp.float32),
        "factors": draw_factors(jax.random.fold_in(splits[3], 71), 0),
    }


def high_dot(left, right):
    return jnp.dot(left, right, precision=lax.Precision.HIGHEST, preferred_element_type=jnp.float32)


def inner_dot(left, right):
    return lax.dot_general(left, right, (((0,), (0,)), ((), ())), precision=lax.Precision.HIGHEST, preferred_element_type=jnp.float32)


def outer_dot(left, right):
    return lax.dot_general(left, right, (((1,), (1,)), ((), ())), precision=lax.Precision.HIGHEST, preferred_element_type=jnp.float32)


def reference(matrix, reflectors, factors):
    current = matrix
    for panel in range(PANELS):
        vectors = reflectors[:, panel * NB:(panel + 1) * NB]
        factor = factors[panel]
        projected = high_dot(high_dot(current, vectors), factor)
        coupling = inner_dot(factor, inner_dot(vectors, projected))
        corrected = projected - 0.5 * high_dot(vectors, coupling)
        current = current - outer_dot(vectors, corrected) - outer_dot(corrected, vectors)
    return current
```

```python
import jax
import jax.numpy as jnp
from jax import lax
from jax.experimental import pallas as pl
from jax.experimental.pallas import tpu as pltpu
from jax.sharding import PartitionSpec as P


AXES = ("prow", "pcol")
BF16 = jnp.bfloat16
F32 = jnp.float32
VMEM_LIMIT = 56 << 20


def contract(left, right, left_dim, right_dim, precision=None):
    return lax.dot_general(
        left,
        right,
        (((left_dim,), (right_dim,)), ((), ())),
        precision=precision,
        preferred_element_type=F32,
    )


def halves(value):
    high = value.astype(BF16)
    return high, (value - high.astype(F32)).astype(BF16)


def contract_split(left, right, left_dim, right_dim):
    left_high, left_low = left
    right_high, right_low = right
    return (
        contract(left_high, right_high, left_dim, right_dim)
        + contract(left_low, right_high, left_dim, right_dim)
        + contract(left_high, right_low, left_dim, right_dim)
    )


def params():
    return pltpu.CompilerParams(vmem_limit_bytes=VMEM_LIMIT)


def partial_kernel(slots_ref, vectors_ref, matrix_ref, out_ref, high_ref, low_ref):
    @pl.when(pl.program_id(0) == 0)
    def _():
        high, low = halves(vectors_ref[...])
        high_ref[...] = high
        low_ref[...] = low

    out_ref[0] = contract_split(
        halves(matrix_ref[...]), (high_ref[...], low_ref[...]), 0, 0
    )


def partial_sums(matrix, reflectors, panel, width, slots, piece):
    rows = matrix.shape[0]
    count = slots.shape[0]
    return pl.pallas_call(
        partial_kernel,
        grid_spec=pltpu.PrefetchScalarGridSpec(
            num_scalar_prefetch=1,
            grid=(count,),
            in_specs=[
                pl.BlockSpec((rows, width), lambda j, s: (0, panel)),
                pl.BlockSpec((rows, piece), lambda j, s: (0, s[j])),
            ],
            out_specs=pl.BlockSpec((1, piece, width), lambda j, s: (j, 0, 0)),
            scratch_shapes=[pltpu.VMEM((rows, width), BF16)] * 2,
        ),
        out_shape=jax.ShapeDtypeStruct((count, piece, width), F32),
        compiler_params=params(),
    )(slots, reflectors, matrix)


def gram_kernel(sums_a_ref, sums_b_ref, vectors_ref, out_ref):
    width = sums_a_ref.shape[1]
    first = halves(vectors_ref[:, :width])
    second_value = vectors_ref[:, width:]
    second = halves(second_value)
    sums_a = halves(sums_a_ref[...])
    sums_b = halves(sums_b_ref[...])
    out_ref[0] = contract_split(first, sums_a, 0, 0)
    out_ref[1] = contract_split(first, sums_b, 0, 0)
    out_ref[2] = contract_split(second, sums_b, 0, 0)
    out_ref[3] = contract_split(first, second, 0, 0)


def grams(sums_a, sums_b, vectors):
    width = sums_a.shape[1]
    return pl.pallas_call(
        gram_kernel,
        out_shape=jax.ShapeDtypeStruct((4, width, width), F32),
        compiler_params=params(),
    )(sums_a, sums_b, vectors)


def small_kernel(gram_ref, factors_ref, x_ref, k_ref):
    width = factors_ref.shape[1]

    def dot(left, right, left_dim=1, right_dim=0):
        return contract(left, right, left_dim, right_dim, lax.Precision.HIGHEST)

    first = factors_ref[0]
    second = factors_ref[1]
    g11 = gram_ref[0]
    g12 = gram_ref[1]
    g22 = gram_ref[2]
    c12 = gram_ref[3]
    m1 = dot(first, dot(g11, first), 0, 0)
    half_m1_c = 0.5 * dot(m1, c12)
    lead = half_m1_c - (dot(first, g12, 0, 0) - 0.5 * dot(m1, c12, 0, 0))
    t1_c = dot(first, c12)
    inner = g22 - dot(g12, t1_c, 0, 0) + dot(c12, lead, 0, 0)
    m2 = dot(second, dot(inner, second), 0, 0)
    x_ref[:width, :width] = first
    x_ref[:width, width:] = -dot(t1_c, second)
    x_ref[width:, :width] = jnp.zeros_like(first)
    x_ref[width:, width:] = second
    cross = dot(lead, second)
    k_ref[:width, :width] = -0.5 * (m1 + m1.T)
    k_ref[:width, width:] = cross
    k_ref[width:, :width] = cross.T
    k_ref[width:, width:] = -0.5 * (m2 + m2.T)


def small(gram, factors):
    width = factors.shape[1]
    shape = jax.ShapeDtypeStruct((2 * width, 2 * width), F32)
    return pl.pallas_call(
        small_kernel, out_shape=(shape, shape), compiler_params=params()
    )(gram, factors)


def column_kernel(row_ref, x_ref, k_ref, *refs):
    own_a, own_b, near_a, near_b, far_a, far_b, high_ref, low_ref = refs
    piece, width = own_a.shape[1:]
    x = halves(x_ref[...])
    k = halves(k_ref[...])
    row = row_ref[0]
    sources = (
        ((own_a, 0), (own_b, 0)),
        ((near_a, 0), (far_b, 0)),
        ((far_a, 0), (near_b, 0)),
        ((far_a, 2), (far_b, 2)),
    )
    for slot, ((left, left_at), (right, right_at)) in enumerate(sources):
        sums = halves(jnp.concatenate([left[left_at], right[right_at]], axis=1))
        vectors = halves(jnp.concatenate([left[left_at + 1], right[right_at + 1]], axis=1))
        first = contract_split(sums, x, 1, 0) + contract_split(vectors, k, 1, 0)
        second = contract_split(vectors, x, 1, 1)
        both = halves(jnp.concatenate([first, second], axis=1))
        at = pl.ds(pl.multiple_of((row ^ slot) * piece, piece), piece)
        high_ref[at, :] = both[0]
        low_ref[at, :] = both[1]


def column_factors(row, x, k, parts, cols):
    width = x.shape[0]
    whole = pl.BlockSpec(memory_space=pltpu.VMEM)
    shape = jax.ShapeDtypeStruct((cols, 2 * width), BF16)
    return pl.pallas_call(
        column_kernel,
        in_specs=[pl.BlockSpec(memory_space=pltpu.SMEM)] + [whole] * (2 + len(parts)),
        out_specs=(whole, whole),
        out_shape=(shape, shape),
        compiler_params=params(),
    )(row, x, k, *parts)


def vector_update_kernel(matrix_ref, vectors_ref, high_ref, low_ref, out_ref):
    out_ref[...] = matrix_ref[...] - contract_split(
        halves(vectors_ref[...]), (high_ref[...], low_ref[...]), 1, 1
    )


def vector_update(matrix, reflectors, high, low, piece):
    rows, cols = matrix.shape
    depth = reflectors.shape[1]
    resident = pl.BlockSpec((cols, depth), lambda j: (0, 0), pipeline_mode=pl.Buffered(1))
    return pl.pallas_call(
        vector_update_kernel,
        grid=(rows // piece,),
        in_specs=[
            pl.BlockSpec((piece, cols), lambda j: (j, 0)),
            pl.BlockSpec((piece, depth), lambda j: (j, 0)),
            resident,
            resident,
        ],
        out_specs=pl.BlockSpec((piece, cols), lambda j: (j, 0)),
        out_shape=jax.ShapeDtypeStruct((rows, cols), F32),
        compiler_params=params(),
    )(matrix, reflectors, high, low)


def sum_update_kernel(block_ref, current_ref, mine_ref, other_ref, high_ref, low_ref, out_ref):
    def update(source):
        out_ref[...] = current_ref[...] - contract_split(
            halves(source[...]), (high_ref[...], low_ref[...]), 1, 1
        )

    pl.when(pl.program_id(0) == 0)(lambda: update(mine_ref))
    pl.when(pl.program_id(0) == 1)(lambda: update(other_ref))


def sum_update(blocks, current, mine, other, high, low):
    rows, cols = current.shape
    piece, depth = mine.shape
    resident = pl.BlockSpec((cols, depth), lambda j, b: (0, 1), pipeline_mode=pl.Buffered(1))
    whole = pl.BlockSpec((piece, depth), lambda j, b: (0, 0), pipeline_mode=pl.Buffered(1))
    tile = pl.BlockSpec((piece, cols), lambda j, b: (b[j], 0))
    return pl.pallas_call(
        sum_update_kernel,
        grid_spec=pltpu.PrefetchScalarGridSpec(
            num_scalar_prefetch=1,
            grid=(2,),
            in_specs=[tile, whole, whole, resident, resident],
            out_specs=tile,
        ),
        out_shape=jax.ShapeDtypeStruct((rows, cols), F32),
        input_output_aliases={1: 0},
        compiler_params=params(),
    )(blocks, current, mine, other, high, low)


def quad_body(matrix, reflectors, factors):
    size = lax.axis_size("prow")
    width = factors.shape[1]
    rows, cols = matrix.shape
    piece = cols // size
    row = lax.axis_index("prow")
    col = lax.axis_index("pcol")
    core = col % 2
    level = col // 2

    def send(value, target):
        pairs = []
        for r in range(size):
            for z in range(size):
                for k in range(2):
                    to = target(r, z, k)
                    if to is not None:
                        source = (r * size + z) * 2 + k
                        pairs.append((source, (to[0] * size + to[1]) * 2 + to[2]))
        return lax.ppermute(value, AXES, pairs)

    def across(step):
        return lambda r, z, k: (r ^ step, z, k)

    def sibling(value):
        return send(value, lambda r, z, k: (r, z, k ^ 1))

    def local_piece(index):
        return lax.dynamic_slice_in_dim(reflectors, core * cols + index * piece, piece, 0)

    vectors = jnp.where(row == level, local_piece(row), jnp.zeros((piece, 2 * width), F32))
    for step in range(1, size):
        vectors = vectors + send(
            local_piece(row ^ step),
            lambda r, z, k, step=step: (r ^ step, z, k) if r == z else None,
        )

    def partial(panel, slots):
        return partial_sums(
            matrix, reflectors, panel, width, jnp.array(slots, jnp.int32) ^ row, piece
        )

    send_a = partial(0, (3, 1))
    got_a = send(send_a, across(1))
    send_b = partial(1, (3, 2))
    got_b = send(send_b, across(2))
    keep_a = partial(0, (2, 0))
    keep_b = partial(1, (1, 0))
    last_a = send(keep_a[0] + got_a[0], across(2))
    last_b = send(keep_b[0] + got_b[0], across(1))
    sums_a = keep_a[1] + got_a[1] + last_a
    sums_b = keep_b[1] + got_b[1] + last_b

    sums = jnp.concatenate([sums_a, sums_b], axis=1)
    direct = [send(sums, lambda r, z, k, q=q: (z, r ^ q, k)) for q in range(size)]
    swapped = [sibling(block) for block in direct]

    own_a = jnp.stack([sums_a, vectors[:, :width]])
    own_b = jnp.stack([sums_b, vectors[:, width:]])
    near_a = send(own_a, across(1))
    near_b = send(own_b, across(2))
    far_a = send(jnp.concatenate([own_a, near_a]), across(2))
    far_b = send(jnp.concatenate([own_b, near_b]), across(1))

    gram = grams(sums_a, sums_b, vectors)
    gram = jnp.where(core == 0, gram[:2], gram[2:]) + sibling(
        jnp.where(core == 0, gram[2:], gram[:2])
    )
    gram = gram.reshape(size, 2 * width // size, width)

    def gram_piece(index):
        return lax.dynamic_index_in_dim(gram, index, 0, keepdims=False)

    part = gram_piece(row)
    for step in range(1, size):
        part = part + send(gram_piece(row ^ step), across(step))
    total = part
    for step in range(1, size):
        total = total + send(part, lambda r, z, k, step=step: (r, z ^ step, k))
    spread = jnp.zeros_like(gram)
    spread = lax.dynamic_update_index_in_dim(spread, total, row, 0)
    for step in range(1, size):
        spread = lax.dynamic_update_index_in_dim(
            spread, send(total, across(step)), row ^ step, 0
        )
    spread = spread.reshape(2, width, width)
    paired = sibling(spread)
    gram = jnp.concatenate(
        [jnp.where(core == 0, spread, paired), jnp.where(core == 0, paired, spread)]
    )
    x, k = small(gram, factors)
    high, low = column_factors(
        row[None], x, k, (own_a, own_b, near_a, near_b, far_a, far_b), cols
    )
    out = vector_update(matrix, reflectors, high, low, piece)
    for q in range(size):
        place = level ^ q
        blocks = jnp.stack([core * size + place, (1 - core) * size + place])
        out = sum_update(blocks, out, direct[q], swapped[q], high, low)
    return out


def spread_block(block, axis, owner):
    block = jnp.where(lax.axis_index(axis) == owner, block, jnp.zeros_like(block))
    return lax.psum(block, axis)


def exact(left, right, left_dim=1, right_dim=0):
    return contract(left, right, left_dim, right_dim, lax.Precision.HIGHEST)


def general_body(matrix, reflectors, factors):
    col_count = matrix.shape[1]
    width = factors.shape[1]
    ratio = lax.axis_size("pcol") // lax.axis_size("prow")
    index = lax.axis_index("pcol")

    def columns(block):
        own = lax.dynamic_slice_in_dim(block, index % ratio * col_count, col_count, 0)
        return spread_block(own, "prow", index // ratio)

    col_vectors = columns(reflectors)
    row_sums = lax.psum(exact(matrix, col_vectors), "pcol")
    col_sums = columns(row_sums)
    first, second = reflectors[:, :width], reflectors[:, width:]
    gram = lax.psum(
        jnp.stack(
            [
                exact(first, row_sums[:, :width], 0, 0),
                exact(first, row_sums[:, width:], 0, 0),
                exact(second, row_sums[:, width:], 0, 0),
                exact(first, second, 0, 0),
            ]
        ),
        "prow",
    )
    x, k = small(gram, factors)
    left = exact(col_sums, x) + exact(col_vectors, k)
    right = exact(col_vectors, x, 1, 1)
    return matrix - exact(reflectors, left, 1, 1) - exact(row_sums, right, 1, 1)


def solution(mesh):
    size = mesh.shape["prow"]

    def body(matrix, reflectors, factors):
        piece = matrix.shape[1] // size
        quad = size == 4 and mesh.shape["pcol"] == 2 * size and piece % 128 == 0
        return (quad_body if quad else general_body)(matrix, reflectors, factors)

    return jax.shard_map(
        body,
        mesh=mesh,
        in_specs=(P("prow", "pcol"), P("prow", None), P()),
        out_specs=P("prow", "pcol"),
        check_vma=False,
    )
```

```python
import functools

import jax
import jax.numpy as jnp
from jax import lax
from jax.experimental import pallas as pl
from jax.experimental.pallas import tpu as pltpu
from jax.sharding import PartitionSpec as P


AXES = ("prow", "pcol")


BF16 = jnp.bfloat16
F32 = jnp.float32
VMEM_LIMIT = 56 << 20


def contract(left, right, left_dim, right_dim, precision=None):
    return lax.dot_general(
        left,
        right,
        (((left_dim,), (right_dim,)), ((), ())),
        precision=precision,
        preferred_element_type=F32,
    )


def halves(value):
    high = value.astype(BF16)
    return high, (value - high.astype(F32)).astype(BF16)


def contract_split(left, right, left_dim, right_dim):
    left_high, left_low = left
    right_high, right_low = right
    return (
        contract(left_high, right_high, left_dim, right_dim)
        + contract(left_low, right_high, left_dim, right_dim)
        + contract(left_high, right_low, left_dim, right_dim)
    )


def params():
    return pltpu.CompilerParams(vmem_limit_bytes=VMEM_LIMIT)


def pair_kernel(slots_ref, vectors_ref, matrix_ref, *refs):
    outs, (high_ref, low_ref) = refs[:-2], refs[-2:]
    width = outs[0].shape[1]

    @pl.when(pl.program_id(0) == 0)
    def _():
        high, low = halves(vectors_ref[...])
        high_ref[...] = high
        low_ref[...] = low

    value = contract_split(halves(matrix_ref[...]), (high_ref[...], low_ref[...]), 0, 0)

    def store(item):
        outs[2 * item][...] = value[:, :width]
        outs[2 * item + 1][...] = value[:, width:]

    for item in range(len(outs) // 2):
        pl.when(pl.program_id(0) == item)(lambda item=item: store(item))


def pair_sums(matrix, reflectors, width, slots, piece):
    rows = matrix.shape[0]
    items = slots.shape[0]
    out = pl.BlockSpec((piece, width), lambda i, s: (0, 0))
    shape = jax.ShapeDtypeStruct((piece, width), F32)
    return pl.pallas_call(
        pair_kernel,
        grid_spec=pltpu.PrefetchScalarGridSpec(
            num_scalar_prefetch=1,
            grid=(items,),
            in_specs=[
                pl.BlockSpec(
                    (rows, 2 * width), lambda i, s: (0, 0), pipeline_mode=pl.Buffered(1)
                ),
                pl.BlockSpec((rows, piece), lambda i, s: (0, s[i])),
            ],
            out_specs=(out,) * (2 * items),
            scratch_shapes=[pltpu.VMEM((rows, 2 * width), BF16)] * 2,
        ),
        out_shape=(shape,) * (2 * items),
        compiler_params=params(),
    )(slots, reflectors, matrix)


def cross_kernel(core_ref, first_ref, second_ref, out_ref):
    out_ref[...] = contract_split(halves(first_ref[...]), halves(second_ref[...]), 0, 0)


def cross_part(core, reflectors, width):
    rows = reflectors.shape[0]
    half = width // 2
    return pl.pallas_call(
        cross_kernel,
        grid_spec=pltpu.PrefetchScalarGridSpec(
            num_scalar_prefetch=1,
            grid=(1,),
            in_specs=[
                pl.BlockSpec((rows, half), lambda i, c: (0, c[0])),
                pl.BlockSpec((rows, width), lambda i, c: (0, 1)),
            ],
            out_specs=pl.BlockSpec((half, width), lambda i, c: (0, 0)),
        ),
        out_shape=jax.ShapeDtypeStruct((half, width), F32),
        compiler_params=params(),
    )(core, reflectors, reflectors)


def gram_kernel(sums_a_ref, sums_b_ref, vectors_ref, out_ref):
    width = sums_a_ref.shape[1]
    first = halves(vectors_ref[:, :width])
    second = halves(vectors_ref[:, width:])
    sums_a = halves(sums_a_ref[...])
    sums_b = halves(sums_b_ref[...])
    out_ref[:width, :] = contract_split(first, sums_a, 0, 0)
    out_ref[width : 2 * width, :] = contract_split(first, sums_b, 0, 0)
    out_ref[2 * width :, :] = contract_split(second, sums_b, 0, 0)


def grams(sums_a, sums_b, vectors):
    width = sums_a.shape[1]
    return pl.pallas_call(
        gram_kernel,
        out_shape=jax.ShapeDtypeStruct((3 * width, width), F32),
        compiler_params=params(),
    )(sums_a, sums_b, vectors)


def exact(left, right, left_dim=1, right_dim=0):
    return contract(left, right, left_dim, right_dim, lax.Precision.HIGHEST)


def mixing(first, second, c12):
    t1_c = exact(first, c12)
    top = jnp.concatenate([first, -exact(t1_c, second)], axis=1)
    bottom = jnp.concatenate([jnp.zeros_like(first), second], axis=1)
    return jnp.concatenate([top, bottom])


def coupling(first, second, c12, g11, g12, g22):
    t1_c = exact(first, c12)
    m1 = exact(first, exact(g11, first), 0, 0)
    half_m1_c = 0.5 * exact(m1, c12)
    lead = half_m1_c - (exact(first, g12, 0, 0) - 0.5 * exact(m1, c12, 0, 0))
    inner = g22 - exact(g12, t1_c, 0, 0) + exact(c12, lead, 0, 0)
    m2 = exact(second, exact(inner, second), 0, 0)
    cross = exact(lead, second)
    top = jnp.concatenate([-0.5 * (m1 + m1.T), cross], axis=1)
    bottom = jnp.concatenate([cross.T, -0.5 * (m2 + m2.T)], axis=1)
    return jnp.concatenate([top, bottom])


def finish_kernel(factors_ref, c12_ref, gram_ref, lead_ref, high_ref, low_ref, *refs):
    out_high, out_low, k_high, k_low = refs
    width = factors_ref.shape[1]

    @pl.when(pl.program_id(0) == 0)
    def _():
        k = coupling(
            factors_ref[0],
            factors_ref[1],
            c12_ref[...],
            gram_ref[:width, :],
            gram_ref[width : 2 * width, :],
            gram_ref[2 * width :, :],
        )
        k_high[...], k_low[...] = halves(k)

    value = lead_ref[...] + contract_split(
        (high_ref[...], low_ref[...]), (k_high[...], k_low[...]), 1, 0
    )
    out_high[...], out_low[...] = halves(value)


def finish_factors(factors, c12, gram, lead, high, low, piece):
    cols, depth = lead.shape
    width = factors.shape[1]
    tile = pl.BlockSpec((piece, depth), lambda j: (j, 0))
    shape = jax.ShapeDtypeStruct((cols, depth), BF16)
    return pl.pallas_call(
        finish_kernel,
        grid=(cols // piece,),
        in_specs=[
            pl.BlockSpec((2, width, width), lambda j: (0, 0, 0)),
            pl.BlockSpec((width, width), lambda j: (0, 0)),
            pl.BlockSpec((3 * width, width), lambda j: (0, 0)),
            tile,
            tile,
            tile,
        ],
        out_specs=(tile, tile),
        out_shape=(shape, shape),
        scratch_shapes=[pltpu.VMEM((depth, depth), BF16)] * 2,
        compiler_params=params(),
    )(factors, c12, gram, lead, high, low)


def slot_pieces(refs):
    own, near_a, near_b, far_a, far_b = refs
    return (
        own[...],
        jnp.concatenate([near_a[...], far_b[0]], axis=1),
        jnp.concatenate([far_a[0], near_b[...]], axis=1),
        jnp.concatenate([far_a[1], far_b[1]], axis=1),
    )


def rows_of(row_ref, slot, piece):
    return pl.ds(pl.multiple_of((row_ref[0] ^ slot) * piece, piece), piece)


def vector_column_kernel(row_ref, factors_ref, c12_ref, *refs):
    right_high, right_low, vector_high, vector_low, x_high, x_low = refs[5:]
    piece = refs[0].shape[0]
    x = halves(mixing(factors_ref[0], factors_ref[1], c12_ref[...]))
    x_high[...], x_low[...] = x
    for slot, value in enumerate(slot_pieces(refs[:5])):
        vectors = halves(value)
        at = rows_of(row_ref, slot, piece)
        right_high[at, :], right_low[at, :] = halves(contract_split(vectors, x, 1, 1))
        vector_high[at, :], vector_low[at, :] = vectors


def sum_column_kernel(row_ref, x_high, x_low, *refs):
    piece = refs[0].shape[0]
    x = (x_high[...], x_low[...])
    for slot, value in enumerate(slot_pieces(refs[:5])):
        refs[5][rows_of(row_ref, slot, piece), :] = contract_split(halves(value), x, 1, 0)


def column_call(kernel, shapes, row, *args):
    whole = pl.BlockSpec(memory_space=pltpu.VMEM)
    return pl.pallas_call(
        kernel,
        in_specs=[pl.BlockSpec(memory_space=pltpu.SMEM)] + [whole] * len(args),
        out_specs=(whole,) * len(shapes),
        out_shape=tuple(jax.ShapeDtypeStruct(*shape) for shape in shapes),
        compiler_params=params(),
    )(row, *args)


def vector_update_kernel(matrix_ref, vectors_ref, high_ref, low_ref, out_ref):
    out_ref[...] = matrix_ref[...] - contract_split(
        halves(vectors_ref[...]), (high_ref[...], low_ref[...]), 1, 1
    )


def vector_update(matrix, reflectors, high, low, piece):
    rows, cols = matrix.shape
    depth = reflectors.shape[1]
    resident = pl.BlockSpec((cols, depth), lambda j: (0, 0), pipeline_mode=pl.Buffered(1))
    return pl.pallas_call(
        vector_update_kernel,
        grid=(rows // piece,),
        in_specs=[
            pl.BlockSpec((piece, cols), lambda j: (j, 0)),
            pl.BlockSpec((piece, depth), lambda j: (j, 0)),
            resident,
            resident,
        ],
        out_specs=pl.BlockSpec((piece, cols), lambda j: (j, 0)),
        out_shape=jax.ShapeDtypeStruct((rows, cols), F32),
        compiler_params=params(),
    )(matrix, reflectors, high, low)


def sum_update_kernel(block_ref, matrix_ref, high_ref, low_ref, *refs, sources):
    out_ref = refs[-1]

    def update(source):
        out_ref[...] = matrix_ref[...] - contract_split(
            halves(source[...]), (high_ref[...], low_ref[...]), 1, 1
        )

    for index in range(sources):
        pl.when(pl.program_id(0) == index)(lambda index=index: update(refs[index]))


def sum_update(blocks, matrix, high, low, sources):
    rows, cols = matrix.shape
    piece, depth = sources[0].shape
    count = len(sources)
    resident = pl.BlockSpec((cols, depth), lambda j, b: (0, 0), pipeline_mode=pl.Buffered(1))
    whole = pl.BlockSpec((piece, depth), lambda j, b: (0, 0), pipeline_mode=pl.Buffered(1))
    tile = pl.BlockSpec((piece, cols), lambda j, b: (b[j], 0))
    return pl.pallas_call(
        functools.partial(sum_update_kernel, sources=count),
        grid_spec=pltpu.PrefetchScalarGridSpec(
            num_scalar_prefetch=1,
            grid=(count,),
            in_specs=[tile, resident, resident]
            + [whole] * count,
            out_specs=tile,
        ),
        out_shape=jax.ShapeDtypeStruct((rows, cols), F32),
        input_output_aliases={1: 0},
        compiler_params=params(),
    )(blocks, matrix, high, low, *sources)


def quad_body(matrix, reflectors, factors):
    size = lax.axis_size("prow")
    width = factors.shape[1]
    _, cols = matrix.shape
    piece = cols // size
    row = lax.axis_index("prow")
    col = lax.axis_index("pcol")
    core = col % 2
    level = col // 2

    def send(value, target):
        pairs = []
        for r in range(size):
            for z in range(size):
                for k in range(2):
                    to = target(r, z, k)
                    if to is not None:
                        source = (r * size + z) * 2 + k
                        pairs.append((source, (to[0] * size + to[1]) * 2 + to[2]))
        return lax.ppermute(value, AXES, pairs)

    def across(step):
        return lambda r, z, k: (r ^ step, z, k)

    def sibling(value):
        return send(value, lambda r, z, k: (r, z, k ^ 1))

    sub = piece // size

    def quarter(index):
        start = core * cols + index * piece + level * sub
        return lax.dynamic_slice_in_dim(reflectors, start, sub, 0)

    def pick(stack, index):
        return lax.dynamic_index_in_dim(stack, index, 0, keepdims=False)

    def pair(slots):
        return pair_sums(
            matrix, reflectors, width, jnp.array(slots, jnp.int32) ^ row, piece
        )

    parts = [quarter(row)]
    for step in range(1, size):
        parts.append(send(quarter(row ^ step), across(step)))
    away = pair((3, 1, 2))
    got_far_a = send(away[0], across(1))
    got_far_b = send(away[1], across(2))
    got_near_a = send(away[2], across(1))
    got_near_b = send(away[5], across(2))
    parts = jnp.stack(parts)
    strips = [pick(parts, row ^ level)]
    for step in range(1, size):
        strips.append(
            send(
                pick(parts, row ^ level ^ step),
                lambda r, z, k, step=step: (r, z ^ step, k),
            )
        )
    own_sum_a, own_sum_b = pair((0,))
    last_a = send(away[4] + got_far_a, across(2))
    last_b = send(away[3] + got_far_b, across(1))
    c12 = cross_part(core[None], reflectors, width)
    strips = jnp.stack(strips)
    vectors = jnp.concatenate([pick(strips, level ^ b) for b in range(size)])
    vectors_a, vectors_b = vectors[:, :width], vectors[:, width:]
    vnear_a = send(vectors_a, across(1))
    vnear_b = send(vectors_b, across(2))
    sums_a = own_sum_a + got_near_a + last_a
    sums_b = own_sum_b + got_near_b + last_b
    sums = jnp.concatenate([sums_a, sums_b], axis=1)
    direct = {}
    for q in (0, 1):
        direct[q] = send(sums, lambda r, z, k, q=q: (z, r ^ q, k))
    gram = grams(sums_a, sums_b, vectors).reshape(2, 3 * width // 2, width)
    gram = pick(gram, core) + sibling(pick(gram, 1 - core))
    gram = gram.reshape(size, 3 * width // (2 * size), width)
    part = pick(gram, row)
    for step in range(1, size):
        part = part + send(pick(gram, row ^ step), across(step))
    c12_half = c12
    for step in range(1, size):
        c12_half = c12_half + send(c12, across(step))
    c12_other = sibling(c12_half)
    c12 = jnp.concatenate(
        [
            jnp.where(core == 0, c12_half, c12_other),
            jnp.where(core == 0, c12_other, c12_half),
        ]
    )
    vfar_a = send(jnp.stack([vectors_a, vnear_a]), across(2))
    vfar_b = send(jnp.stack([vectors_b, vnear_b]), across(1))
    near_a = send(sums_a, across(1))
    near_b = send(sums_b, across(2))
    total = part
    for step in range(1, size):
        total = total + send(part, lambda r, z, k, step=step: (r, z ^ step, k))
    pieces = jnp.stack([total] + [send(total, across(step)) for step in range(1, size)])
    spread = jnp.concatenate([pick(pieces, row ^ b) for b in range(size)])
    for q in (2, 3):
        direct[q] = send(sums, lambda r, z, k, q=q: (z, r ^ q, k))
    far_a = send(jnp.stack([sums_a, near_a]), across(2))
    far_b = send(jnp.stack([sums_b, near_b]), across(1))
    paired = sibling(spread)
    gram = jnp.concatenate(
        [jnp.where(core == 0, spread, paired), jnp.where(core == 0, paired, spread)]
    )
    depth = 2 * width
    wide, tall = ((depth, depth), BF16), ((cols, depth), BF16)
    right_high, right_low, vector_high, vector_low, x_high, x_low = column_call(
        vector_column_kernel, (tall,) * 4 + (wide,) * 2, row[None],
        factors, c12, vectors, vnear_a, vnear_b, vfar_a, vfar_b,
    )
    (lead,) = column_call(
        sum_column_kernel, (((cols, depth), F32),), row[None],
        x_high, x_low, sums, near_a, near_b, far_a, far_b,
    )
    high, low = finish_factors(factors, c12, gram, lead, vector_high, vector_low, piece)
    out = vector_update(matrix, reflectors, high, low, piece)
    swapped = [sibling(direct[q]) for q in range(size)]
    for half, sources in (
        (core, [direct[q] for q in range(size)]), (1 - core, swapped)
    ):
        blocks = jnp.stack([half * size + (level ^ q) for q in range(size)])
        out = sum_update(blocks, out, right_high, right_low, sources)
    return out


def spread_block(block, axis, owner):
    block = jnp.where(lax.axis_index(axis) == owner, block, jnp.zeros_like(block))
    return lax.psum(block, axis)


def general_body(matrix, reflectors, factors):
    col_count = matrix.shape[1]
    width = factors.shape[1]
    ratio = lax.axis_size("pcol") // lax.axis_size("prow")
    index = lax.axis_index("pcol")

    def columns(block):
        own = lax.dynamic_slice_in_dim(block, index % ratio * col_count, col_count, 0)
        return spread_block(own, "prow", index // ratio)

    col_vectors = columns(reflectors)
    row_sums = lax.psum(exact(matrix, col_vectors), "pcol")
    col_sums = columns(row_sums)
    first, second = reflectors[:, :width], reflectors[:, width:]
    gram = lax.psum(
        jnp.stack(
            [
                exact(first, row_sums[:, :width], 0, 0),
                exact(first, row_sums[:, width:], 0, 0),
                exact(second, row_sums[:, width:], 0, 0),
                exact(first, second, 0, 0),
            ]
        ),
        "prow",
    )
    x = mixing(factors[0], factors[1], gram[3])
    k = coupling(factors[0], factors[1], gram[3], gram[0], gram[1], gram[2])
    left = exact(col_sums, x) + exact(col_vectors, k)
    right = exact(col_vectors, x, 1, 1)
    return matrix - exact(reflectors, left, 1, 1) - exact(row_sums, right, 1, 1)


def solution(mesh):
    size = mesh.shape["prow"]

    def body(matrix, reflectors, factors):
        piece = matrix.shape[1] // size
        quad = size == 4 and mesh.shape["pcol"] == 2 * size and piece % 128 == 0 and piece % (8 * size) == 0
        return (quad_body if quad else general_body)(matrix, reflectors, factors)

    return jax.shard_map(
        body,
        mesh=mesh,
        in_specs=(P("prow", "pcol"), P("prow", None), P()),
        out_specs=P("prow", "pcol"),
        check_vma=False,
    )
```

```python
import functools

import jax
import jax.numpy as jnp
from jax import lax
from jax.experimental import pallas as pl
from jax.experimental.pallas import tpu as pltpu
from jax.sharding import PartitionSpec as P


AXES = ("prow", "pcol")


BF16 = jnp.bfloat16
F32 = jnp.float32
VMEM_LIMIT = 56 << 20


def contract(left, right, left_dim, right_dim, precision=None):
    return lax.dot_general(
        left,
        right,
        (((left_dim,), (right_dim,)), ((), ())),
        precision=precision,
        preferred_element_type=F32,
    )


def halves(value):
    high = value.astype(BF16)
    return high, (value - high.astype(F32)).astype(BF16)


def contract_split(left, right, left_dim, right_dim):
    left_high, left_low = left
    right_high, right_low = right
    return (
        contract(left_high, right_high, left_dim, right_dim)
        + contract(left_low, right_high, left_dim, right_dim)
        + contract(left_high, right_low, left_dim, right_dim)
    )


def params():
    return pltpu.CompilerParams(vmem_limit_bytes=VMEM_LIMIT)


def pair_kernel(slots_ref, vectors_ref, matrix_ref, *refs):
    outs, (high_ref, low_ref) = refs[:-2], refs[-2:]
    width = outs[0].shape[1]

    @pl.when(pl.program_id(0) == 0)
    def _():
        high, low = halves(vectors_ref[...])
        high_ref[...] = high
        low_ref[...] = low

    value = contract_split(halves(matrix_ref[...]), (high_ref[...], low_ref[...]), 0, 0)

    def store(item):
        outs[2 * item][...] = value[:, :width]
        outs[2 * item + 1][...] = value[:, width:]

    for item in range(len(outs) // 2):
        pl.when(pl.program_id(0) == item)(lambda item=item: store(item))


def pair_sums(matrix, reflectors, width, slots, piece):
    rows = matrix.shape[0]
    items = slots.shape[0]
    out = pl.BlockSpec((piece, width), lambda i, s: (0, 0))
    shape = jax.ShapeDtypeStruct((piece, width), F32)
    return pl.pallas_call(
        pair_kernel,
        grid_spec=pltpu.PrefetchScalarGridSpec(
            num_scalar_prefetch=1,
            grid=(items,),
            in_specs=[
                pl.BlockSpec(
                    (rows, 2 * width), lambda i, s: (0, 0), pipeline_mode=pl.Buffered(1)
                ),
                pl.BlockSpec((rows, piece), lambda i, s: (0, s[i])),
            ],
            out_specs=(out,) * (2 * items),
            scratch_shapes=[pltpu.VMEM((rows, 2 * width), BF16)] * 2,
        ),
        out_shape=(shape,) * (2 * items),
        compiler_params=params(),
    )(slots, reflectors, matrix)


def cross_kernel(core_ref, first_ref, second_ref, out_ref):
    out_ref[...] = contract_split(halves(first_ref[...]), halves(second_ref[...]), 0, 0)


def cross_part(core, reflectors, width):
    rows = reflectors.shape[0]
    half = width // 2
    return pl.pallas_call(
        cross_kernel,
        grid_spec=pltpu.PrefetchScalarGridSpec(
            num_scalar_prefetch=1,
            grid=(1,),
            in_specs=[
                pl.BlockSpec((rows, half), lambda i, c: (0, c[0])),
                pl.BlockSpec((rows, width), lambda i, c: (0, 1)),
            ],
            out_specs=pl.BlockSpec((half, width), lambda i, c: (0, 0)),
        ),
        out_shape=jax.ShapeDtypeStruct((half, width), F32),
        compiler_params=params(),
    )(core, reflectors, reflectors)


def gram_kernel(sums_a_ref, sums_b_ref, vectors_ref, out_ref):
    width = sums_a_ref.shape[1]
    first = halves(vectors_ref[:, :width])
    second = halves(vectors_ref[:, width:])
    sums_a = halves(sums_a_ref[...])
    sums_b = halves(sums_b_ref[...])
    out_ref[:width, :] = contract_split(first, sums_a, 0, 0)
    out_ref[width : 2 * width, :] = contract_split(first, sums_b, 0, 0)
    out_ref[2 * width :, :] = contract_split(second, sums_b, 0, 0)


def grams(sums_a, sums_b, vectors):
    width = sums_a.shape[1]
    return pl.pallas_call(
        gram_kernel,
        out_shape=jax.ShapeDtypeStruct((3 * width, width), F32),
        compiler_params=params(),
    )(sums_a, sums_b, vectors)


def exact(left, right, left_dim=1, right_dim=0):
    return contract(left, right, left_dim, right_dim, lax.Precision.HIGHEST)


def mixing(first, second, c12):
    t1_c = exact(first, c12)
    top = jnp.concatenate([first, -exact(t1_c, second)], axis=1)
    bottom = jnp.concatenate([jnp.zeros_like(first), second], axis=1)
    return jnp.concatenate([top, bottom])


def coupling(first, second, c12, g11, g12, g22, dot):
    t1_c = dot(first, c12)
    m1 = dot(first, dot(g11, first), 0, 0)
    half_m1_c = 0.5 * dot(m1, c12)
    lead = half_m1_c - (dot(first, g12, 0, 0) - 0.5 * dot(m1, c12, 0, 0))
    inner = g22 - dot(g12, t1_c, 0, 0) + dot(c12, lead, 0, 0)
    m2 = dot(second, dot(inner, second), 0, 0)
    cross = dot(lead, second)
    top = jnp.concatenate([-0.5 * (m1 + m1.T), cross], axis=1)
    bottom = jnp.concatenate([cross.T, -0.5 * (m2 + m2.T)], axis=1)
    return jnp.concatenate([top, bottom])


def split_dot(left, right, left_dim=1, right_dim=0):
    return contract_split(halves(left), halves(right), left_dim, right_dim)


def choose_kernel(index_ref, *refs, count):
    sources, outs, held_ref = refs[:-1 - count], refs[-1 - count : -1], refs[-1]
    for number, source in enumerate(sources):

        @pl.when(index_ref[pl.program_id(0)] == number)
        def _(source=source):
            held_ref[...] = source[...]

    for number, out in enumerate(outs):

        @pl.when(pl.program_id(0) == number)
        def _(out=out):
            out[...] = held_ref[...]


def choose(index, sources):
    count = index.shape[0]
    shape = sources[0].shape
    whole = pl.BlockSpec(shape, lambda j, i: (0, 0), pipeline_mode=pl.Buffered(1))
    return pl.pallas_call(
        functools.partial(choose_kernel, count=count),
        grid_spec=pltpu.PrefetchScalarGridSpec(
            num_scalar_prefetch=1,
            grid=(count,),
            in_specs=[whole] * len(sources),
            out_specs=(pl.BlockSpec(shape, lambda j, i: (0, 0)),) * count,
            scratch_shapes=[pltpu.VMEM(shape, F32)],
        ),
        out_shape=(jax.ShapeDtypeStruct(shape, F32),) * count,
        compiler_params=params(),
    )(index, *sources)


def finish_kernel(row_ref, factors_ref, c12_ref, gram_ref, x_high, x_low, *refs):
    vector_high, vector_low, out_high, out_low, k_high, k_low, sums_ref = refs[5:]
    width = factors_ref.shape[1]
    slot = pl.program_id(0)

    @pl.when(slot == 0)
    def _():
        k = coupling(
            factors_ref[0],
            factors_ref[1],
            c12_ref[...],
            gram_ref[:width, :],
            gram_ref[width : 2 * width, :],
            gram_ref[2 * width :, :],
            split_dot,
        )
        k_high[...], k_low[...] = halves(k)

    for index, parts in enumerate(slot_refs(refs[:5])):

        @pl.when(slot == index)
        def _(parts=parts):
            at = 0
            for ref, lead in parts:
                value = ref[...] if lead is None else ref[lead]
                sums_ref[:, at : at + value.shape[1]] = value
                at += value.shape[1]

    value = contract_split(
        halves(sums_ref[...]), (x_high[...], x_low[...]), 1, 0
    ) + contract_split(
        (vector_high[...], vector_low[...]), (k_high[...], k_low[...]), 1, 0
    )
    out_high[...], out_low[...] = halves(value)


def finish_factors(row, factors, c12, gram, x_high, x_low, parts, high, low, piece):
    cols, depth = high.shape
    tile = pl.BlockSpec((piece, depth), lambda j, r: (r[0] ^ j, 0))
    shape = jax.ShapeDtypeStruct((cols, depth), BF16)
    whole = pl.BlockSpec(memory_space=pltpu.VMEM)
    return pl.pallas_call(
        finish_kernel,
        grid_spec=pltpu.PrefetchScalarGridSpec(
            num_scalar_prefetch=1,
            grid=(cols // piece,),
            in_specs=[whole] * (5 + len(parts)) + [tile, tile],
            out_specs=(tile, tile),
            scratch_shapes=[pltpu.VMEM((depth, depth), BF16)] * 2
            + [pltpu.VMEM((piece, depth), F32)],
        ),
        out_shape=(shape, shape),
        compiler_params=params(),
    )(row, factors, c12, gram, x_high, x_low, *parts, high, low)


def slot_refs(refs):
    own, near_a, near_b, far_a, far_b = refs
    return (
        ((own, None),),
        ((near_a, None), (far_b, 0)),
        ((far_a, 0), (near_b, None)),
        ((far_a, 1), (far_b, 1)),
    )


def slot_pieces(refs):
    own, near_a, near_b, far_a, far_b = refs
    return (
        own[...],
        jnp.concatenate([near_a[...], far_b[0]], axis=1),
        jnp.concatenate([far_a[0], near_b[...]], axis=1),
        jnp.concatenate([far_a[1], far_b[1]], axis=1),
    )


def rows_of(row_ref, slot, piece):
    return pl.ds(pl.multiple_of((row_ref[0] ^ slot) * piece, piece), piece)


def vector_column_kernel(row_ref, factors_ref, c12_ref, *refs):
    right_high, right_low, vector_high, vector_low, x_high, x_low = refs[5:]
    piece = refs[0].shape[0]
    x = halves(mixing(factors_ref[0], factors_ref[1], c12_ref[...]))
    x_high[...], x_low[...] = x
    for slot, value in enumerate(slot_pieces(refs[:5])):
        vectors = halves(value)
        at = rows_of(row_ref, slot, piece)
        right_high[at, :], right_low[at, :] = halves(contract_split(vectors, x, 1, 1))
        vector_high[at, :], vector_low[at, :] = vectors


def column_call(kernel, shapes, row, *args):
    whole = pl.BlockSpec(memory_space=pltpu.VMEM)
    return pl.pallas_call(
        kernel,
        in_specs=[pl.BlockSpec(memory_space=pltpu.SMEM)] + [whole] * len(args),
        out_specs=(whole,) * len(shapes),
        out_shape=tuple(jax.ShapeDtypeStruct(*shape) for shape in shapes),
        compiler_params=params(),
    )(row, *args)


def vector_update_kernel(matrix_ref, vectors_ref, high_ref, low_ref, out_ref):
    out_ref[...] = matrix_ref[...] - contract_split(
        halves(vectors_ref[...]), (high_ref[...], low_ref[...]), 1, 1
    )


def vector_update(matrix, reflectors, high, low, piece):
    rows, cols = matrix.shape
    depth = reflectors.shape[1]
    resident = pl.BlockSpec((cols, depth), lambda j: (0, 0), pipeline_mode=pl.Buffered(1))
    return pl.pallas_call(
        vector_update_kernel,
        grid=(rows // piece,),
        in_specs=[
            pl.BlockSpec((piece, cols), lambda j: (j, 0)),
            pl.BlockSpec((piece, depth), lambda j: (j, 0)),
            resident,
            resident,
        ],
        out_specs=pl.BlockSpec((piece, cols), lambda j: (j, 0)),
        out_shape=jax.ShapeDtypeStruct((rows, cols), F32),
        compiler_params=params(),
    )(matrix, reflectors, high, low)


def sum_update_kernel(block_ref, matrix_ref, high_ref, low_ref, *refs, sources):
    out_ref = refs[-1]

    def update(source):
        out_ref[...] = matrix_ref[...] - contract_split(
            halves(source[...]), (high_ref[...], low_ref[...]), 1, 1
        )

    for index in range(sources):
        pl.when(pl.program_id(0) == index)(lambda index=index: update(refs[index]))


def sum_update(blocks, matrix, high, low, sources):
    rows, cols = matrix.shape
    piece, depth = sources[0].shape
    count = len(sources)
    resident = pl.BlockSpec((cols, depth), lambda j, b: (0, 0), pipeline_mode=pl.Buffered(1))
    whole = pl.BlockSpec((piece, depth), lambda j, b: (0, 0), pipeline_mode=pl.Buffered(1))
    tile = pl.BlockSpec((piece, cols), lambda j, b: (b[j], 0))
    return pl.pallas_call(
        functools.partial(sum_update_kernel, sources=count),
        grid_spec=pltpu.PrefetchScalarGridSpec(
            num_scalar_prefetch=1,
            grid=(count,),
            in_specs=[tile, resident, resident]
            + [whole] * count,
            out_specs=tile,
        ),
        out_shape=jax.ShapeDtypeStruct((rows, cols), F32),
        input_output_aliases={1: 0},
        compiler_params=params(),
    )(blocks, matrix, high, low, *sources)


def quad_body(matrix, reflectors, factors):
    size = lax.axis_size("prow")
    width = factors.shape[1]
    _, cols = matrix.shape
    piece = cols // size
    row = lax.axis_index("prow")
    col = lax.axis_index("pcol")
    core = col % 2
    level = col // 2

    def send(value, target):
        pairs = []
        for r in range(size):
            for z in range(size):
                for k in range(2):
                    to = target(r, z, k)
                    if to is not None:
                        source = (r * size + z) * 2 + k
                        pairs.append((source, (to[0] * size + to[1]) * 2 + to[2]))
        return lax.ppermute(value, AXES, pairs)

    def across(step):
        return lambda r, z, k: (r ^ step, z, k)

    def sibling(value):
        return send(value, lambda r, z, k: (r, z, k ^ 1))

    sub = piece // size

    def quarter(index):
        start = core * cols + index * piece + level * sub
        return lax.dynamic_slice_in_dim(reflectors, start, sub, 0)

    def pick(stack, index):
        return lax.dynamic_index_in_dim(stack, index, 0, keepdims=False)

    def pair(slots):
        return pair_sums(
            matrix, reflectors, width, jnp.array(slots, jnp.int32) ^ row, piece
        )

    parts = [quarter(row)]
    for step in range(1, size):
        parts.append(send(quarter(row ^ step), across(step)))
    away = pair((3, 1, 2))
    got_far_a = send(away[0], across(1))
    got_far_b = send(away[1], across(2))
    got_near_a = send(away[2], across(1))
    got_near_b = send(away[5], across(2))
    parts = jnp.stack(parts)
    strips = [pick(parts, row ^ level)]
    for step in range(1, size):
        strips.append(
            send(
                pick(parts, row ^ level ^ step),
                lambda r, z, k, step=step: (r, z ^ step, k),
            )
        )
    own_sum_a, own_sum_b = pair((0,))
    last_a = send(away[4] + got_far_a, across(2))
    last_b = send(away[3] + got_far_b, across(1))
    c12 = cross_part(core[None], reflectors, width)
    strips = jnp.stack(strips)
    vectors = jnp.concatenate([pick(strips, level ^ b) for b in range(size)])
    vectors_a, vectors_b = vectors[:, :width], vectors[:, width:]
    vnear_a = send(vectors_a, across(1))
    vnear_b = send(vectors_b, across(2))
    sums_a = own_sum_a + got_near_a + last_a
    sums_b = own_sum_b + got_near_b + last_b
    sums = jnp.concatenate([sums_a, sums_b], axis=1)
    ups, downs = [sums], [sums]
    for step in range(1, size):
        ups.append(
            send(
                ups[-1],
                lambda r, z, k, step=step: (r, z + 1, k)
                if step - 1 <= z < size - 1
                else None,
            )
        )
        downs.append(
            send(
                downs[-1],
                lambda r, z, k, step=step: (r, z - 1, k)
                if 0 < z <= size - step
                else None,
            )
        )
    gram = grams(sums_a, sums_b, vectors).reshape(2, 3 * width // 2, width)
    gram = pick(gram, core) + sibling(pick(gram, 1 - core))
    gram = gram.reshape(size, 3 * width // (2 * size), width)
    part = pick(gram, row)
    for step in range(1, size):
        part = part + send(pick(gram, row ^ step), across(step))
    c12_half = c12
    for step in range(1, size):
        c12_half = c12_half + send(c12, across(step))
    c12_other = sibling(c12_half)
    c12 = jnp.concatenate(
        [
            jnp.where(core == 0, c12_half, c12_other),
            jnp.where(core == 0, c12_other, c12_half),
        ]
    )
    vfar_a = send(jnp.stack([vectors_a, vnear_a]), across(2))
    vfar_b = send(jnp.stack([vectors_b, vnear_b]), across(1))
    near_a = send(sums_a, across(1))
    near_b = send(sums_b, across(2))
    total = part
    for step in range(1, size):
        total = total + send(part, lambda r, z, k, step=step: (r, z ^ step, k))
    pieces = jnp.stack([total] + [send(total, across(step)) for step in range(1, size)])
    spread = jnp.concatenate([pick(pieces, row ^ b) for b in range(size)])
    far_a = send(jnp.stack([sums_a, near_a]), across(2))
    far_b = send(jnp.stack([sums_b, near_b]), across(1))
    paired = sibling(spread)
    gram = jnp.concatenate(
        [jnp.where(core == 0, spread, paired), jnp.where(core == 0, paired, spread)]
    )
    depth = 2 * width
    wide, tall = ((depth, depth), BF16), ((cols, depth), BF16)
    right_high, right_low, vector_high, vector_low, x_high, x_low = column_call(
        vector_column_kernel, (tall,) * 4 + (wide,) * 2, row[None],
        factors, c12, vectors, vnear_a, vnear_b, vfar_a, vfar_b,
    )
    high, low = finish_factors(
        row[None], factors, c12, gram, x_high, x_low,
        (sums, near_a, near_b, far_a, far_b), vector_high, vector_low, piece,
    )
    out = vector_update(matrix, reflectors, high, low, piece)
    wanted = (jnp.arange(size, dtype=jnp.int32) ^ row) - level + size - 1
    chosen = choose(wanted, ups[:0:-1] + [sums] + downs[1:])
    direct = [chosen[0]] + [send(chosen[m], across(m)) for m in range(1, size)]
    swapped = [sibling(direct[q]) for q in range(size)]
    for half, sources in (
        (core, [direct[q] for q in range(size)]), (1 - core, swapped)
    ):
        blocks = jnp.stack([half * size + (row ^ m) for m in range(size)])
        out = sum_update(blocks, out, right_high, right_low, sources)
    return out


def spread_block(block, axis, owner):
    block = jnp.where(lax.axis_index(axis) == owner, block, jnp.zeros_like(block))
    return lax.psum(block, axis)


def general_body(matrix, reflectors, factors):
    col_count = matrix.shape[1]
    width = factors.shape[1]
    ratio = lax.axis_size("pcol") // lax.axis_size("prow")
    index = lax.axis_index("pcol")

    def columns(block):
        own = lax.dynamic_slice_in_dim(block, index % ratio * col_count, col_count, 0)
        return spread_block(own, "prow", index // ratio)

    col_vectors = columns(reflectors)
    row_sums = lax.psum(exact(matrix, col_vectors), "pcol")
    col_sums = columns(row_sums)
    first, second = reflectors[:, :width], reflectors[:, width:]
    gram = lax.psum(
        jnp.stack(
            [
                exact(first, row_sums[:, :width], 0, 0),
                exact(first, row_sums[:, width:], 0, 0),
                exact(second, row_sums[:, width:], 0, 0),
                exact(first, second, 0, 0),
            ]
        ),
        "prow",
    )
    x = mixing(factors[0], factors[1], gram[3])
    k = coupling(
        factors[0], factors[1], gram[3], gram[0], gram[1], gram[2], exact
    )
    left = exact(col_sums, x) + exact(col_vectors, k)
    right = exact(col_vectors, x, 1, 1)
    return matrix - exact(reflectors, left, 1, 1) - exact(row_sums, right, 1, 1)


def solution(mesh):
    size = mesh.shape["prow"]

    def body(matrix, reflectors, factors):
        piece = matrix.shape[1] // size
        quad = size == 4 and mesh.shape["pcol"] == 2 * size and piece % 128 == 0 and piece % (8 * size) == 0
        return (quad_body if quad else general_body)(matrix, reflectors, factors)

    return jax.shard_map(
        body,
        mesh=mesh,
        in_specs=(P("prow", "pcol"), P("prow", None), P()),
        out_specs=P("prow", "pcol"),
        check_vma=False,
    )
```
